32 devices in a mesh: leaf: 32 (over z, y, x, core).
Axes of the slice: x: 2, y: 2, z: 4, core: 2. Of those that a mesh axis runs over, the one named last changes fastest.
Arguments:
- points: bfloat16 [65536, 128], P('leaf'), may hold values from -6 to 6
- charges: bfloat16 [65536, 256], P('leaf'), may hold values from -6 to 6
- order: int32 [32, 2048], P('leaf'), may hold values from 0 to 2047, each once within a row
- near: int32 [32, 2], P('leaf'), may hold values from 0 to 31, as said below
- bases: bfloat16 [65536, 256], P('leaf'), may hold values from -0.125 to 0.125
- lift_leaf: float32 [8192, 256], P('leaf'), may hold values from -0.1875 to 0.1875
- lift_node: float32 [2048, 256], P('leaf'), may hold values from -0.1875 to 0.1875
- proxy_leaf: float32 [8192, 128], P('leaf'), may hold values from -5 to 5
- proxy_node: float32 [2048, 128], P('leaf'), may hold values from -5 to 5
- proxy_top: float32 [512, 128], P('leaf'), may hold values from -5 to 5
Outputs:
- potential: bfloat16 [65536, 256], P('leaf')
The draws below stay inside these ranges and needn't reach their ends.
Inputs may be any that keep to these rules, and one draw needn't show every extreme that they name: `order`: each row is a permutation of the leaf's 2048 positions. `near`: row l names two distinct leaves other than l from l's aligned group of four leaves; the relation is symmetric, and the group's remaining leaf is l's far partner, whose index differs from l in exactly one of the two lowest bits.
All inputs are finite; a program needn't handle non-finite values.
Results may differ from the reference program's by a relative error of at most 0.0049.
Values may be sent and summed in bfloat16 or wider, within the bound.
A program may use at most 64 MiB of HBM per device.

```python
import jax
import jax.numpy as jnp
from jax import lax

D = 128
NRHS = 256
RANK = 256
LEAF = 2048
NPTS = 65536
TOPN = 2
N_LEAF = 32


def draw_near(key, part):
    drawn_bits = jax.random.randint(key, (N_LEAF // 4,), 1, 3)
    group_ids = jnp.arange(N_LEAF // 4, dtype=jnp.int32)
    partner_bits = jnp.where(group_ids % 2 == 0, 2, drawn_bits).astype(jnp.int32)
    leaf_ids = jnp.arange(N_LEAF, dtype=jnp.int32)
    leaf_slot = leaf_ids % 4
    spread = jnp.repeat(partner_bits, 4).astype(jnp.int32)
    first_bits = jnp.where(spread == 1, 2, 1).astype(jnp.int32)
    second_bits = jnp.full((N_LEAF,), 3, jnp.int32)
    start = leaf_ids - leaf_slot
    first_near = start + jnp.bitwise_xor(leaf_slot, first_bits)
    second_near = start + jnp.bitwise_xor(leaf_slot, second_bits)
    return jnp.stack([first_near, second_near], axis=1).astype(jnp.int32)


def level_offset(key, salt):
    offset_key = jax.random.fold_in(key, salt)
    sign_key, size_key = jax.random.split(offset_key)
    signs = jnp.where(jax.random.bernoulli(sign_key, 0.5, (D,)), 1.0, -1.0).astype(jnp.float32)
    sizes = jax.random.uniform(size_key, (D,), jnp.float32, 0.45, 0.75)
    return signs * sizes


def normal_proxy(key, rows, salt):
    offset = level_offset(key, salt)
    noise = 0.75 * jax.random.normal(jax.random.fold_in(key, salt + 1), (rows, D), jnp.float32)
    return jnp.clip(offset[None, :] + noise, -5.0, 5.0).astype(jnp.float32)


def draw_proxy_leaf(key, part):
    return normal_proxy(key, N_LEAF * RANK, 101)


def draw_proxy_node(key, part):
    return normal_proxy(key, N_LEAF // 4 * RANK, 203)


def draw_proxy_top(key, part):
    return normal_proxy(key, TOPN * RANK, 307)


def steps_of(stream_key, dims, cuts, low, largest):
    loudness, own = 1.0, jax.random.fold_in(stream_key, 6)
    for dim, blocks in cuts:
        draws = jnp.exp(jax.random.uniform(jax.random.fold_in(own, dim), (blocks,), jnp.float32, low / len(cuts), largest / len(cuts)))
        loudness = loudness * jnp.repeat(draws, dims[dim] // blocks).reshape([-1 if axis == dim else 1 for axis in range(len(dims))])
    return loudness


def centred(key, shape, scale, most, cuts=(), held_as=jnp.bfloat16):
    values = scale * jax.random.normal(key, shape, jnp.float32)
    if cuts:
        values = values * steps_of(key, shape, cuts, -0.22, 0.18)
    return jnp.clip(values, -most, most).astype(held_as)


def setup_inputs(seed: int = 0) -> dict:
    streams_of = jax.random.split(jax.random.key(seed), 11)
    return {
        "points": centred(streams_of[0], (NPTS, D), 1.0, 6.0, ((0, 32),)),
        "charges": centred(streams_of[1], (NPTS, NRHS), 1.0, 6.0, ((0, 32),)),
        "order": jax.vmap(lambda own: jax.random.permutation(own, LEAF))(jax.random.split(streams_of[2], N_LEAF)).reshape((N_LEAF, LEAF)).astype(jnp.int32),
        "near": draw_near(jax.random.fold_in(streams_of[10], 71), 0),
        "bases": centred(streams_of[4], (NPTS, RANK), LEAF ** -0.5, 0.125, ((0, 32),)),
        "lift_leaf": centred(streams_of[5], (N_LEAF * RANK, RANK), (4 * RANK) ** -0.5, 0.1875, ((0, 32),), jnp.float32),
        "lift_node": centred(streams_of[6], (N_LEAF // 4 * RANK, RANK), (4 * RANK) ** -0.5, 0.1875, ((0, 32),), jnp.float32),
        "proxy_leaf": draw_proxy_leaf(jax.random.fold_in(streams_of[10], 71), 0),
        "proxy_node": draw_proxy_node(jax.random.fold_in(streams_of[10], 71), 0),
        "proxy_top": draw_proxy_top(jax.random.fold_in(streams_of[10], 71), 0),
    }


highest = lax.Precision.HIGHEST


def kernel_tile(left, right):
    products = jnp.dot(left, right.T, preferred_element_type=jnp.float32)
    left_norm = jnp.sum(jnp.square(left.astype(jnp.float32)), axis=1)
    right_norm = jnp.sum(jnp.square(right.astype(jnp.float32)), axis=1)
    return jnp.exp((2.0 * products - left_norm[:, None] - right_norm[None, :]) * (2.0 / D))


def couple(left, right):
    products = jnp.dot(left, right.T, precision=highest)
    left_norm = jnp.sum(left * left, axis=1)
    right_norm = jnp.sum(right * right, axis=1)
    return jnp.exp((2.0 * products - left_norm[:, None] - right_norm[None, :]) * (2.0 / D))


def reference(points, charges, order, near, bases, lift_leaf, lift_node, proxy_leaf, proxy_node, proxy_top):
    leaf_points = points.reshape(N_LEAF, LEAF, D)
    leaf_rhs = jnp.take_along_axis(charges.reshape(N_LEAF, LEAF, NRHS), order[:, :, None], axis=1)
    leaf_bases = bases.reshape(N_LEAF, LEAF, RANK)

    def near_leaf(leaf_id):
        total = jnp.zeros((LEAF, NRHS), jnp.float32)
        own = leaf_points[leaf_id]
        for source in (leaf_id, near[leaf_id, 0], near[leaf_id, 1]):
            tile = kernel_tile(own, leaf_points[source]).astype(jnp.bfloat16)
            total = total + jnp.dot(tile, leaf_rhs[source], preferred_element_type=jnp.float32)
        return total

    near_sum = lax.map(near_leaf, jnp.arange(N_LEAF, dtype=jnp.int32))

    def leaf_coeff(pair):
        return lax.dot_general(pair[0], pair[1], (((0,), (0,)), ((), ())), preferred_element_type=jnp.float32)

    coefficient = lax.map(leaf_coeff, (leaf_bases, leaf_rhs))
    lifts = lift_leaf.reshape(N_LEAF, RANK, RANK)
    upward = jnp.einsum("lkr,lkc->lrc", lifts, coefficient, precision=highest)
    node_coeff = upward.reshape(N_LEAF // 4, 4, RANK, NRHS).sum(axis=1)
    node_lifts = lift_node.reshape(N_LEAF // 4, RANK, RANK)
    top_coeff = jnp.einsum("gkr,gkc->grc", node_lifts, node_coeff, precision=highest)
    top_coeff = top_coeff.reshape(TOPN, 4, RANK, NRHS).sum(axis=1)
    leaf_proxy = proxy_leaf.reshape(N_LEAF, RANK, D)
    node_proxy = proxy_node.reshape(N_LEAF // 4, RANK, D)
    top_flat = top_coeff.reshape(TOPN * RANK, NRHS)
    owner = jnp.arange(TOPN * RANK, dtype=jnp.int32) // RANK

    def top_field(node):
        kernel = couple(lax.dynamic_slice_in_dim(proxy_top, node * RANK, RANK, 0), proxy_top)
        kernel = jnp.where(owner[None, :] != node, kernel, 0.0)
        return jnp.dot(kernel, top_flat, precision=highest)

    field_top = lax.map(top_field, jnp.arange(TOPN, dtype=jnp.int32))
    group_proxy = node_proxy.reshape(N_LEAF // 16, 4 * RANK, D)
    group_coeff = node_coeff.reshape(N_LEAF // 16, 4 * RANK, NRHS)
    sibling_owner = jnp.arange(4 * RANK, dtype=jnp.int32) // RANK

    def node_field(node):
        kernel = couple(node_proxy[node], group_proxy[node // 4])
        kernel = jnp.where(sibling_owner[None, :] != node % 4, kernel, 0.0)
        far_part = jnp.dot(kernel, group_coeff[node // 4], precision=highest)
        return far_part + jnp.dot(node_lifts[node], field_top[node // 4], precision=highest)

    field_node = lax.map(node_field, jnp.arange(N_LEAF // 4, dtype=jnp.int32))
    group_leaf_proxy = leaf_proxy.reshape(N_LEAF // 4, 4 * RANK, D)
    group_leaf_coeff = coefficient.reshape(N_LEAF // 4, 4 * RANK, NRHS)

    def leaf_field(leaf_id):
        partner = 6 - leaf_id % 4 - near[leaf_id, 0] % 4 - near[leaf_id, 1] % 4
        kernel = couple(leaf_proxy[leaf_id], group_leaf_proxy[leaf_id // 4])
        kernel = jnp.where(sibling_owner[None, :] == partner, kernel, 0.0)
        far_part = jnp.dot(kernel, group_leaf_coeff[leaf_id // 4], precision=highest)
        far_part = far_part + jnp.dot(lifts[leaf_id], field_node[leaf_id // 4], precision=highest)
        return far_part.astype(jnp.bfloat16)

    field_leaf = lax.map(leaf_field, jnp.arange(N_LEAF, dtype=jnp.int32))

    def descend(pair):
        return jnp.dot(pair[0], pair[1], preferred_element_type=jnp.float32)

    descent = lax.map(descend, (leaf_bases, field_leaf))
    return (near_sum + descent).astype(jnp.bfloat16).reshape(N_LEAF * LEAF, NRHS)
```

```python
import functools

import jax
import jax.numpy as jnp
from jax import lax
from jax.experimental import pallas as pl
from jax.experimental.pallas import tpu as pltpu
from jax.sharding import PartitionSpec as P

MESH = pl.DeviceIdType.MESH
F32, BF16 = jnp.float32, jnp.bfloat16
CHUNKS = 8
EARLY = 5
ROWS = 512


def mm(a, b, ca=1, cb=0):
    return lax.dot_general(a, b, (((ca,), (cb,)), ((), ())), preferred_element_type=F32)


def split3(x):
    high = x.astype(BF16).astype(F32)
    middle = (x - high).astype(BF16).astype(F32)
    return high, middle, x - high - middle


def norm_column(p):
    wide = p.astype(F32)
    return jnp.sum(wide * wide, axis=1, keepdims=True)


def norm_lanes(p, one_scale, norm_scale, norm_first):
    high, middle, low = split3(norm_column(p))
    lane = lax.broadcasted_iota(jnp.int32, (p.shape[0], 128), 1)
    first = 0 if norm_first else 3
    ones = jnp.where(lane < 6, one_scale, 0.0)
    out = jnp.where(lane == first, high * norm_scale, ones)
    out = jnp.where(lane == first + 1, middle * norm_scale, out)
    out = jnp.where(lane == first + 2, low * norm_scale, out)
    return out.astype(BF16)


def couple(left, right):
    scale = 2.0 / left.shape[1]
    wide = right.astype(F32)
    square = wide * wide
    high = square.astype(BF16)
    low = (square - high.astype(F32)).astype(BF16)
    ones = jnp.ones((8, left.shape[1]), BF16)
    right_norm = (mm(ones, high, 1, 1) + mm(ones, low, 1, 1))[0:1, :]
    return jnp.exp((2.0 * mm(left, right, 1, 1) - norm_column(left) - right_norm) * scale).astype(BF16)


def kernel(n, near, points, charges, order, bases, lift, nlift, zleaf, znode, ztop, out,
           rhs, laug, raug, acc, p1, p2, p3, r1, r2, r3, cp, cr,
           c0, c0x, z0, z0x, ut, rs, nl, z1, z1s, z2, nv, nvs, c2, c2o, z2o, f1,
           ssem, rsem):
    me = lax.axis_index("leaf")
    leaf, dim = points.shape
    rank = lift.shape[0]
    quarter = rank // 4
    sixteenth = rank // 16
    nodes = n // 16
    slot = me % 4
    group = me // 4 % 4
    part = me % 16
    node = me // 16
    step = leaf // CHUNKS

    def flip(bits):
        if bits == 1:
            return me + 1 - 2 * (me % 2)
        if bits == 2:
            return me + 2 - 4 * (me // 2 % 2)
        if bits == 3:
            return me - slot + 3 - slot
        if bits == 4:
            return me + 4 - 8 * (me // 4 % 2)
        if bits == 8:
            return me + 8 - 16 * (me // 8 % 2)
        return me - 4 * group + 4 * (3 - group)

    def flip_slot(bits):
        if bits == 1:
            return slot + 1 - 2 * (slot % 2)
        if bits == 2:
            return slot + 2 - 4 * (slot // 2)
        return 3 - slot

    others = [(node + d) % nodes * 16 + part for d in range(1, nodes)]

    barrier = pltpu.get_barrier_semaphore()
    partners = [flip(b) for b in (1, 2, 3, 4, 8, 12)] + others
    for other in partners:
        pl.semaphore_signal(barrier, inc=1, device_id=(other,), device_id_type=MESH)

    count = [0]
    started = []

    def send(src, dst, device):
        i = count[0]
        count[0] += 1
        copy = pltpu.make_async_remote_copy(
            src_ref=src, dst_ref=dst, send_sem=ssem.at[i], recv_sem=rsem.at[i],
            device_id=(device,), device_id_type=MESH)
        copy.start()
        started.append(copy)
        return copy

    mine = pl.ds(pl.multiple_of(slot * quarter, quarter), quarter)
    mine16 = pl.ds(pl.multiple_of(part * sixteenth, sixteenth), sixteenth)
    mine64 = pl.ds(pl.multiple_of(group * quarter, quarter), quarter)
    z1[mine, :] = znode[...].astype(BF16)
    nl[mine, :] = nlift[...].astype(BF16)
    z2[mine16, :] = ztop[...].astype(BF16)
    z0[...] = zleaf[...].astype(BF16)
    pl.semaphore_wait(barrier, len(partners))

    points_one = send(points, p1, flip(1))
    points_two = send(points, p2, flip(2))
    phase_a = []
    for b in (1, 2, 3):
        phase_a.append(send(z1.at[mine, :], z1.at[mine, :], flip(b)))
        phase_a.append(send(nl.at[mine, :], nl.at[mine, :], flip(b)))
        phase_a.append(send(z2.at[mine16, :], z2.at[mine16, :], flip(b)))

    def permute(block, carry):
        rows = pl.ds(pl.multiple_of(block * 128, 128), 128)
        index = jnp.broadcast_to(order[0:1, rows].astype(F32), (128, 128)).T
        lane = lax.broadcasted_iota(jnp.int32, (128, 128), 1).astype(F32)
        chosen = jnp.concatenate(
            [jnp.where(index == lane + 128.0 * j, 1.0, 0.0).astype(BF16) for j in range(leaf // 128)], 1)
        rhs[rows, :] = mm(chosen, charges[...]).astype(BF16)
        return carry

    lax.fori_loop(0, leaf // 128, permute, 0)

    own = mm(rhs[...], bases[...], 0, 0).astype(BF16)
    c0[...] = own
    lift16 = lift[...].astype(BF16)
    up = mm(own, lift16)
    ut[...] = up.astype(BF16)
    phase_up = []
    for b in (1, 2, 3):
        there = pl.ds(pl.multiple_of(flip_slot(b) * quarter, quarter), quarter)
        phase_up.append(send(ut.at[there, :], rs.at[b - 1], flip(b)))
    rhs_one = send(rhs, r1, flip(1))
    rhs_two = []

    def send_chunk(c):
        rows = pl.ds(c * step, step)
        rhs_two.append(send(rhs.at[rows, :], r2.at[rows, :], flip(2)))

    phase_far = []
    send_chunk(0)
    for b in (1, 2):
        phase_far.append(send(c0, c0x.at[b - 1], flip(b)))
        phase_far.append(send(z0, z0x.at[b - 1], flip(b)))
    for c in range(1, EARLY):
        send_chunk(c)

    def augment(block, carry):
        rows = pl.ds(pl.multiple_of(block * ROWS, ROWS), ROWS)
        p = points[rows, :]
        laug[rows, 0:dim] = (p.astype(F32) * (4.0 / dim)).astype(BF16)
        laug[rows, dim:] = norm_lanes(p, -2.0 / dim, -2.0 / dim, False)
        raug[rows, 0:dim] = p
        raug[rows, dim:] = norm_lanes(p, 1.0, 1.0, True)
        return carry

    lax.fori_loop(0, leaf // ROWS, augment, 0)

    def tiles(rows, right, width):
        left = laug[rows, :]
        return jnp.concatenate(
            [jnp.exp(mm(left, right[j:j + 512, :], 1, 1)).astype(BF16) for j in range(0, width, 512)], 1)

    def own_tile(block, carry):
        rows = pl.ds(pl.multiple_of(block * ROWS, ROWS), ROWS)
        acc[rows, :] = mm(tiles(rows, raug, leaf), rhs[...])
        return carry

    blocks = leaf // ROWS
    lax.fori_loop(0, blocks // 2, own_tile, 0)

    for copy in phase_a:
        copy.wait_recv()
    phase_b = []
    for i, b in enumerate((4, 8, 12)):
        phase_b.append(send(z1, z1s.at[i], flip(b)))
        phase_b.append(send(z2.at[mine64, :], z2.at[mine64, :], flip(b)))
    for copy in phase_up:
        copy.wait_recv()
    total = ut[mine, :].astype(F32)
    for i in range(3):
        total = total + rs[i].astype(F32)
    nv[0] = total.astype(BF16)
    lifted = mm(total.astype(BF16), nl[...])
    nv[1] = lifted.astype(BF16)
    phase_two = [send(nv, nvs.at[i], flip(b)) for i, b in enumerate((4, 8, 12))]

    lax.fori_loop(blocks // 2, blocks, own_tile, 0)

    points_two.wait_recv()
    points_three = send(p2, p3, flip(1))
    for copy in phase_b:
        copy.wait_recv()
    for copy in phase_two:
        copy.wait_recv()
    for i in range(3):
        lifted = lifted + nvs[i, 1].astype(F32)
    c2[...] = lifted.astype(BF16)
    phase_top = []
    for d, other in enumerate(others):
        phase_top.append(send(c2, c2o.at[d], other))
        phase_top.append(send(z2, z2o.at[d], other))

    side = mm(nvs[0, 0], couple(z1s[0], z1[...]))
    for i in (1, 2):
        side = side + mm(nvs[i, 0], couple(z1s[i], z1[...]))

    first = near[0, 0] - me
    second = near[0, 1] - me
    one = 1 - 2 * (me % 2)
    near_one = jnp.logical_or(first == one, second == one)

    def choose(a, b):
        return jnp.where(near_one, a.astype(F32), b.astype(F32)).astype(BF16)

    phase_rhs = []

    def relay(c):
        rhs_two[c].wait_recv()
        rows = pl.ds(c * step, step)
        phase_rhs.append(send(r2.at[rows, :], r3.at[rows, :], flip(1)))

    def near_chunk(c, final):
        rows = pl.ds(c * step, step)
        phase_rhs[c].wait_recv()
        picked = choose(p1[rows, :], p2[rows, :])
        cp[0:step, 0:dim] = picked
        cp[0:step, dim:] = norm_lanes(picked, 1.0, 1.0, True)
        diagonal = p3[rows, :]
        cp[step:, 0:dim] = diagonal
        cp[step:, dim:] = norm_lanes(diagonal, 1.0, 1.0, True)
        cr[0:step, :] = choose(r1[rows, :], r2[rows, :])
        cr[step:, :] = r3[rows, :]

        def body(block, carry):
            rows = pl.ds(pl.multiple_of(block * ROWS, ROWS), ROWS)
            value = acc[rows, :] + mm(tiles(rows, cp, 2 * step), cr[...])
            if final:
                out[rows, :] = value.astype(BF16)
            else:
                acc[rows, :] = value
            return carry

        lax.fori_loop(0, blocks, body, 0)

    relay(0)
    rhs_one.wait_recv()
    points_one.wait_recv()
    for copy in phase_top:
        copy.wait_recv()
    field = mm(c2o[0], couple(z2o[0], z2[...]))
    for d in range(1, nodes - 1):
        field = field + mm(c2o[d], couple(z2o[d], z2[...]))
    field1 = side + mm(field.astype(BF16), nl[...], 1, 1)
    f1[mine, :] = field1.astype(BF16)
    phase_down = [send(f1.at[mine, :], f1.at[mine, :], flip(b)) for b in (1, 2, 3)]
    for c in range(EARLY, CHUNKS):
        send_chunk(c)
    points_three.wait_recv()
    for c in range(1, CHUNKS):
        relay(c)
        near_chunk(c - 1, False)
        if c == 5:
            for copy in phase_far:
                copy.wait_recv()
            for copy in phase_down:
                copy.wait_recv()
            far_z = choose(z0x[1], z0x[0])
            far_c = choose(c0x[1], c0x[0])
            field0 = mm(far_c, couple(far_z, z0[...])) + mm(f1[...], lift[...].astype(BF16), 1, 1)
            c0x[0] = field0.astype(BF16)

            def descend(block, carry):
                rows = pl.ds(pl.multiple_of(block * ROWS, ROWS), ROWS)
                acc[rows, :] += mm(bases[rows, :], c0x[0], 1, 1)
                return carry

            lax.fori_loop(0, blocks, descend, 0)
    near_chunk(CHUNKS - 1, True)
    for copy in started:
        copy.wait_send()


def per_device(n, near, points, charges, order, bases, lift, nlift, zleaf, znode, ztop):
    leaf, dim = points.shape
    nrhs = charges.shape[1]
    rank = lift.shape[0]
    quarter = rank // 4
    nodes = n // 16
    copies = 11 + 3 + 1 + CHUNKS + 4 + 6 + 3 + 1 + 2 * (nodes - 1) + CHUNKS + 3
    v = pltpu.VMEM
    vmem = pl.BlockSpec(memory_space=pltpu.VMEM)
    return pl.pallas_call(
        functools.partial(kernel, n),
        out_shape=jax.ShapeDtypeStruct((leaf, nrhs), BF16),
        in_specs=[pl.BlockSpec(memory_space=pltpu.SMEM)] + [vmem] * 9,
        out_specs=vmem,
        scratch_shapes=[
            v((leaf, nrhs), BF16), v((leaf, 2 * dim), BF16), v((leaf, 2 * dim), BF16),
            v((leaf, nrhs), F32),
            v((leaf, dim), BF16), v((leaf, dim), BF16), v((leaf, dim), BF16),
            v((leaf, nrhs), BF16), v((leaf, nrhs), BF16), v((leaf, nrhs), BF16),
            v((2 * leaf // CHUNKS, 2 * dim), BF16), v((2 * leaf // CHUNKS, nrhs), BF16),
            v((nrhs, rank), BF16), v((2, nrhs, rank), BF16),
            v((rank, dim), BF16), v((2, rank, dim), BF16),
            v((nrhs, rank), BF16), v((3, quarter, rank), BF16),
            v((rank, rank), BF16), v((rank, dim), BF16), v((3, rank, dim), BF16),
            v((rank, dim), BF16),
            v((2, quarter, rank), BF16), v((3, 2, quarter, rank), BF16),
            v((quarter, rank), BF16), v((nodes - 1, quarter, rank), BF16),
            v((nodes - 1, rank, dim), BF16), v((nrhs, rank), BF16),
            pltpu.SemaphoreType.DMA((copies,)), pltpu.SemaphoreType.DMA((copies,)),
        ],
        compiler_params=pltpu.CompilerParams(
            collective_id=0, has_side_effects=True, vmem_limit_bytes=60 * 1024 * 1024),
    )(near, points, charges, order, bases, lift, nlift, zleaf, znode, ztop)


def solution(mesh):
    n = mesh.shape["leaf"]

    def body(points, charges, order, near, bases, lift, nlift, zleaf, znode, ztop):
        return per_device(n, near, points, charges, order, bases, lift, nlift, zleaf, znode, ztop)

    return jax.shard_map(
        body, mesh=mesh, in_specs=(P("leaf", None),) * 10, out_specs=P("leaf", None), check_vma=False)
```

```python
import functools

import jax
import jax.numpy as jnp
from jax import lax
from jax.experimental import pallas as pl
from jax.experimental.pallas import tpu as pltpu
from jax.sharding import PartitionSpec as P

MESH = pl.DeviceIdType.MESH
F32, BF16 = jnp.float32, jnp.bfloat16
CHUNKS = 8
EARLY = 6
ROWS = 512


def mm(a, b, ca=1, cb=0):
    return lax.dot_general(a, b, (((ca,), (cb,)), ((), ())), preferred_element_type=F32)


def split3(x):
    high = x.astype(BF16).astype(F32)
    middle = (x - high).astype(BF16).astype(F32)
    return high, middle, x - high - middle


def norm_column(p):
    wide = p.astype(F32)
    return jnp.sum(wide * wide, axis=1, keepdims=True)


def norm_lanes(p, one_scale, norm_scale, norm_first):
    high, middle, low = split3(norm_column(p))
    lane = lax.broadcasted_iota(jnp.int32, (p.shape[0], 128), 1)
    first = 0 if norm_first else 3
    ones = jnp.where(lane < 6, one_scale, 0.0)
    out = jnp.where(lane == first, high * norm_scale, ones)
    out = jnp.where(lane == first + 1, middle * norm_scale, out)
    out = jnp.where(lane == first + 2, low * norm_scale, out)
    return out.astype(BF16)


def couple(left, right):
    scale = 2.0 / left.shape[1]
    wide = right.astype(F32)
    square = wide * wide
    high = square.astype(BF16)
    low = (square - high.astype(F32)).astype(BF16)
    ones = jnp.ones((8, left.shape[1]), BF16)
    right_norm = (mm(ones, high, 1, 1) + mm(ones, low, 1, 1))[0:1, :]
    return jnp.exp((2.0 * mm(left, right, 1, 1) - norm_column(left) - right_norm) * scale).astype(BF16)


def kernel(n, near, points_in, charges_in, bases_in, order, lift, nlift, zleaf, znode, ztop, out,
           points, charges, bases, rhs, laug, raug, acc, p1, p2, p3, r1, r2, r3, cp, cr,
           c0, c0x, z0, z0x, ut, us, rs, nl, z1, z1s, z2, nv, nvs, c2, c2o, z2o, f1,
           ssem, rsem, lsem):
    me = lax.axis_index("leaf")
    leaf, dim = points.shape
    rank = lift.shape[0]
    quarter = rank // 4
    head = leaf * 3 // 4
    sixteenth = rank // 16
    nodes = n // 16
    slot = me % 4
    group = me // 4 % 4
    part = me % 16
    node = me // 16
    step = leaf // CHUNKS

    def flip(bits):
        if bits == 1:
            return me + 1 - 2 * (me % 2)
        if bits == 2:
            return me + 2 - 4 * (me // 2 % 2)
        if bits == 3:
            return me - slot + 3 - slot
        if bits == 4:
            return me + 4 - 8 * (me // 4 % 2)
        if bits == 8:
            return me + 8 - 16 * (me // 8 % 2)
        return me - 4 * group + 4 * (3 - group)

    def flip_slot(bits):
        if bits == 1:
            return slot + 1 - 2 * (slot % 2)
        if bits == 2:
            return slot + 2 - 4 * (slot // 2)
        return 3 - slot

    others = [(node + d) % nodes * 16 + part for d in range(1, nodes)]

    barrier = pltpu.get_barrier_semaphore()
    partners = [flip(b) for b in (1, 2, 3, 4, 8, 12)] + others
    for other in partners:
        pl.semaphore_signal(barrier, inc=1, device_id=(other,), device_id_type=MESH)

    loads = [pltpu.make_async_copy(a, b, lsem.at[i]) for i, (a, b) in enumerate(
        ((charges_in, charges), (bases_in, bases), (points_in, points)))]
    for copy in loads:
        copy.start()
    count = [0]
    started = []

    def send(src, dst, device):
        i = count[0]
        count[0] += 1
        copy = pltpu.make_async_remote_copy(
            src_ref=src, dst_ref=dst, send_sem=ssem.at[i], recv_sem=rsem.at[i],
            device_id=(device,), device_id_type=MESH)
        copy.start()
        started.append(copy)
        return copy

    mine = pl.ds(pl.multiple_of(slot * quarter, quarter), quarter)
    mine16 = pl.ds(pl.multiple_of(part * sixteenth, sixteenth), sixteenth)
    mine64 = pl.ds(pl.multiple_of(group * quarter, quarter), quarter)
    z1[mine, :] = znode[...].astype(BF16)
    nl[mine, :] = nlift[...].astype(BF16)
    z2[mine16, :] = ztop[...].astype(BF16)
    z0[...] = zleaf[...].astype(BF16)
    pl.semaphore_wait(barrier, len(partners))

    def at_slot(bits):
        where = flip_slot(bits) if bits else slot
        return pl.ds(pl.multiple_of(where * quarter, quarter), quarter)

    far16 = pl.ds(pl.multiple_of(flip(2) % 16 * sixteenth, sixteenth), sixteenth)
    phase_a2 = [send(z1.at[mine, :], z1.at[mine, :], flip(2)),
                send(nl.at[mine, :], nl.at[mine, :], flip(2)),
                send(z2.at[mine16, :], z2.at[mine16, :], flip(2))]
    top, rest = pl.ds(0, head), pl.ds(head, leaf - head)
    points_two = send(points_in.at[top, :], p2.at[top, :], flip(2))
    phase_a = [send(z1.at[mine, :], z1.at[mine, :], flip(1)),
               send(nl.at[mine, :], nl.at[mine, :], flip(1)),
               send(z2.at[mine16, :], z2.at[mine16, :], flip(1))]
    points_one = send(points_in, p1, flip(1))
    loads[0].wait()

    def permute(block, carry):
        rows = pl.ds(pl.multiple_of(block * 128, 128), 128)
        index = jnp.broadcast_to(order[0:1, rows].astype(F32), (128, 128)).T
        lane = lax.broadcasted_iota(jnp.int32, (128, 128), 1).astype(F32)
        chosen = jnp.concatenate(
            [jnp.where(index == lane + 128.0 * j, 1.0, 0.0).astype(BF16) for j in range(leaf // 128)], 1)
        rhs[rows, :] = mm(chosen, charges[...]).astype(BF16)
        return carry

    lax.fori_loop(0, leaf // 128, permute, 0)

    loads[1].wait()
    own = mm(rhs[...], bases[...], 0, 0).astype(BF16)
    c0[...] = own
    up = mm(own, lift[...].astype(BF16))
    ut[...] = up.astype(BF16)
    up_near = send(ut.at[at_slot(1), :], rs.at[0], flip(1))
    up_cross = send(ut.at[at_slot(3), :], rs.at[1], flip(1))
    rhs_one = send(rhs, r1, flip(1))
    for copy in phase_a2:
        copy.wait_recv()
    phase_a.append(send(z1.at[at_slot(2), :], z1.at[at_slot(2), :], flip(1)))
    phase_a.append(send(nl.at[at_slot(2), :], nl.at[at_slot(2), :], flip(1)))
    phase_a.append(send(z2.at[far16, :], z2.at[far16, :], flip(1)))
    rhs_two = []

    def send_chunk(c):
        rows = pl.ds(c * step, step)
        rhs_two.append(send(rhs.at[rows, :], r2.at[rows, :], flip(2)))

    loads[2].wait()
    up_cross.wait_recv()
    us[...] = (ut[at_slot(2), :].astype(F32) + rs[1].astype(F32)).astype(BF16)
    up_two = send(us, rs.at[2], flip(2))
    points_rest = send(points_in.at[rest, :], p2.at[rest, :], flip(2))
    send_chunk(0)
    send_chunk(1)
    phase_far = []
    for b in (1, 2):
        phase_far.append(send(c0, c0x.at[b - 1], flip(b)))
        phase_far.append(send(z0, z0x.at[b - 1], flip(b)))
    for c in range(2, EARLY):
        send_chunk(c)

    def augment(block, carry):
        rows = pl.ds(pl.multiple_of(block * ROWS, ROWS), ROWS)
        p = points[rows, :]
        laug[rows, 0:dim] = (p.astype(F32) * (4.0 / dim)).astype(BF16)
        laug[rows, dim:] = norm_lanes(p, -2.0 / dim, -2.0 / dim, False)
        raug[rows, 0:dim] = p
        raug[rows, dim:] = norm_lanes(p, 1.0, 1.0, True)
        return carry

    lax.fori_loop(0, leaf // ROWS, augment, 0)

    def tiles(rows, right, width):
        left = laug[rows, :]
        return jnp.concatenate(
            [jnp.exp(mm(left, right[j:j + 512, :], 1, 1)).astype(BF16) for j in range(0, width, 512)], 1)

    def own_tile(block, carry):
        rows = pl.ds(pl.multiple_of(block * ROWS, ROWS), ROWS)
        acc[rows, :] = mm(tiles(rows, raug, leaf), rhs[...])
        return carry

    blocks = leaf // ROWS
    for copy in phase_a:
        copy.wait_recv()
    phase_b = []
    for i, b in enumerate((4, 8, 12)):
        phase_b.append(send(z1, z1s.at[i], flip(b)))
        phase_b.append(send(z2.at[mine64, :], z2.at[mine64, :], flip(b)))

    lax.fori_loop(0, blocks // 2, own_tile, 0, unroll=2)

    up_near.wait_recv()
    up_two.wait_recv()
    total = ut[mine, :].astype(F32) + rs[0].astype(F32) + rs[2].astype(F32)
    nv[0] = total.astype(BF16)
    lifted = mm(total.astype(BF16), nl[...])
    nv[1] = lifted.astype(BF16)
    phase_two = [send(nv, nvs.at[i], flip(b)) for i, b in enumerate((4, 8, 12))]
    points_two.wait_recv()
    points_three = [send(p2.at[top, :], p3.at[top, :], flip(1))]

    lax.fori_loop(blocks // 2, blocks, own_tile, 0, unroll=2)

    for copy in phase_b:
        copy.wait_recv()
    for copy in phase_two:
        copy.wait_recv()
    for i in range(3):
        lifted = lifted + nvs[i, 1].astype(F32)
    c2[...] = lifted.astype(BF16)
    phase_top = []
    for d, other in enumerate(others):
        phase_top.append(send(c2, c2o.at[d], other))
        phase_top.append(send(z2, z2o.at[d], other))
    points_rest.wait_recv()
    points_three.append(send(p2.at[rest, :], p3.at[rest, :], flip(1)))

    side = mm(nvs[0, 0], couple(z1s[0], z1[...]))
    for i in (1, 2):
        side = side + mm(nvs[i, 0], couple(z1s[i], z1[...]))

    first = near[0, 0] - me
    second = near[0, 1] - me
    one = 1 - 2 * (me % 2)
    near_one = jnp.logical_or(first == one, second == one)

    def choose(a, b):
        return jnp.where(near_one, a.astype(F32), b.astype(F32)).astype(BF16)

    phase_rhs = []

    def relay(c):
        rhs_two[c].wait_recv()
        rows = pl.ds(c * step, step)
        phase_rhs.append(send(r2.at[rows, :], r3.at[rows, :], flip(1)))

    def near_chunk(c, final):
        rows = pl.ds(c * step, step)
        phase_rhs[c].wait_recv()
        picked = choose(p1[rows, :], p2[rows, :])
        cp[0:step, 0:dim] = picked
        cp[0:step, dim:] = norm_lanes(picked, 1.0, 1.0, True)
        diagonal = p3[rows, :]
        cp[step:, 0:dim] = diagonal
        cp[step:, dim:] = norm_lanes(diagonal, 1.0, 1.0, True)
        cr[0:step, :] = choose(r1[rows, :], r2[rows, :])
        cr[step:, :] = r3[rows, :]

        def body(block, carry):
            rows = pl.ds(pl.multiple_of(block * ROWS, ROWS), ROWS)
            value = acc[rows, :] + mm(tiles(rows, cp, 2 * step), cr[...])
            if final:
                out[rows, :] = value.astype(BF16)
            else:
                acc[rows, :] = value
            return carry

        lax.fori_loop(0, blocks, body, 0, unroll=2)

    relay(0)
    rhs_one.wait_recv()
    points_one.wait_recv()
    for copy in points_three:
        copy.wait_recv()
    relay(1)
    near_chunk(0, False)
    for copy in phase_top:
        copy.wait_recv()
    field = mm(c2o[0], couple(z2o[0], z2[...]))
    for d in range(1, nodes - 1):
        field = field + mm(c2o[d], couple(z2o[d], z2[...]))
    field1 = side + mm(field.astype(BF16), nl[...], 1, 1)
    f1[mine, :] = field1.astype(BF16)
    down_two = send(f1.at[mine, :], f1.at[mine, :], flip(2))
    phase_down = [send(f1.at[mine, :], f1.at[mine, :], flip(1))]
    for c in range(EARLY, CHUNKS):
        send_chunk(c)
    for c in range(2, CHUNKS):
        relay(c)
        near_chunk(c - 1, False)
        if c == CHUNKS - 2:
            down_two.wait_recv()
            phase_down.append(send(f1.at[at_slot(2), :], f1.at[at_slot(2), :], flip(1)))
        if c == CHUNKS - 1:
            for copy in phase_far:
                copy.wait_recv()
            for copy in phase_down:
                copy.wait_recv()
            far_z = choose(z0x[1], z0x[0])
            far_c = choose(c0x[1], c0x[0])
            field0 = mm(far_c, couple(far_z, z0[...])) + mm(f1[...], lift[...].astype(BF16), 1, 1)
            c0x[0] = field0.astype(BF16)

            def descend(block, carry):
                rows = pl.ds(pl.multiple_of(block * ROWS, ROWS), ROWS)
                acc[rows, :] += mm(bases[rows, :], c0x[0], 1, 1)
                return carry

            lax.fori_loop(0, blocks, descend, 0)
    near_chunk(CHUNKS - 1, True)
    for copy in started:
        copy.wait_send()


def per_device(n, near, points, charges, order, bases, lift, nlift, zleaf, znode, ztop):
    leaf, dim = points.shape
    nrhs = charges.shape[1]
    rank = lift.shape[0]
    quarter = rank // 4
    nodes = n // 16
    copies = 8 + 2 + 1 + 3 + 2 + CHUNKS + 4 + 6 + 3 + 2 + 2 * (nodes - 1) + CHUNKS + 3
    v = pltpu.VMEM
    vmem = pl.BlockSpec(memory_space=pltpu.VMEM)
    return pl.pallas_call(
        functools.partial(kernel, n),
        out_shape=jax.ShapeDtypeStruct((leaf, nrhs), BF16),
        in_specs=[pl.BlockSpec(memory_space=pltpu.SMEM)] + [pl.BlockSpec(memory_space=pl.ANY)] * 3 + [vmem] * 6,
        out_specs=vmem,
        scratch_shapes=[
            v((leaf, dim), BF16), v((leaf, nrhs), BF16), v((leaf, rank), BF16),
            v((leaf, nrhs), BF16), v((leaf, 2 * dim), BF16), v((leaf, 2 * dim), BF16),
            v((leaf, nrhs), F32),
            v((leaf, dim), BF16), v((leaf, dim), BF16), v((leaf, dim), BF16),
            v((leaf, nrhs), BF16), v((leaf, nrhs), BF16), v((leaf, nrhs), BF16),
            v((2 * leaf // CHUNKS, 2 * dim), BF16), v((2 * leaf // CHUNKS, nrhs), BF16),
            v((nrhs, rank), BF16), v((2, nrhs, rank), BF16),
            v((rank, dim), BF16), v((2, rank, dim), BF16),
            v((nrhs, rank), BF16), v((quarter, rank), BF16), v((3, quarter, rank), BF16),
            v((rank, rank), BF16), v((rank, dim), BF16), v((3, rank, dim), BF16),
            v((rank, dim), BF16),
            v((2, quarter, rank), BF16), v((3, 2, quarter, rank), BF16),
            v((quarter, rank), BF16), v((nodes - 1, quarter, rank), BF16),
            v((nodes - 1, rank, dim), BF16), v((nrhs, rank), BF16),
            pltpu.SemaphoreType.DMA((copies,)), pltpu.SemaphoreType.DMA((copies,)),
            pltpu.SemaphoreType.DMA((3,)),
        ],
        compiler_params=pltpu.CompilerParams(
            collective_id=0, has_side_effects=True, vmem_limit_bytes=60 * 1024 * 1024),
    )(near, points, charges, bases, order, lift, nlift, zleaf, znode, ztop)


def solution(mesh):
    n = mesh.shape["leaf"]

    def body(points, charges, order, near, bases, lift, nlift, zleaf, znode, ztop):
        return per_device(n, near, points, charges, order, bases, lift, nlift, zleaf, znode, ztop)

    return jax.shard_map(
        body, mesh=mesh, in_specs=(P("leaf", None),) * 10, out_specs=P("leaf", None), check_vma=False)
```

```python
import functools

import jax
import jax.numpy as jnp
from jax import lax
from jax.experimental import pallas as pl
from jax.experimental.pallas import tpu as pltpu
from jax.sharding import PartitionSpec as P

MESH = pl.DeviceIdType.MESH
F32, BF16 = jnp.float32, jnp.bfloat16
CHUNKS = 8
EARLY = 6
ROWS = 1024


def mm(a, b, ca=1, cb=0):
    return lax.dot_general(a, b, (((ca,), (cb,)), ((), ())), preferred_element_type=F32)


def split3(x):
    high = x.astype(BF16).astype(F32)
    middle = (x - high).astype(BF16).astype(F32)
    return high, middle, x - high - middle


def norm_column(p):
    wide = p.astype(F32)
    return jnp.sum(wide * wide, axis=1, keepdims=True)


def norm_lanes(p, one_scale, norm_scale, norm_first):
    high, middle, low = split3(norm_column(p))
    lane = lax.broadcasted_iota(jnp.int32, (p.shape[0], 128), 1)
    first = 0 if norm_first else 3
    ones = jnp.where(lane < 6, one_scale, 0.0)
    out = jnp.where(lane == first, high * norm_scale, ones)
    out = jnp.where(lane == first + 1, middle * norm_scale, out)
    out = jnp.where(lane == first + 2, low * norm_scale, out)
    return out.astype(BF16)


def couple(left, right):
    scale = 2.0 / left.shape[1]
    wide = right.astype(F32)
    square = wide * wide
    high = square.astype(BF16)
    low = (square - high.astype(F32)).astype(BF16)
    ones = jnp.ones((8, left.shape[1]), BF16)
    right_norm = (mm(ones, high, 1, 1) + mm(ones, low, 1, 1))[0:1, :]
    return jnp.exp((2.0 * mm(left, right, 1, 1) - norm_column(left) - right_norm) * scale).astype(BF16)


def kernel(n, near, points_in, charges_in, bases_in, order, lift, nlift, zleaf, znode, ztop, out,
           points, charges, bases, rhs, laug, raug, acc, p1, p2, p3, r1, r2, r3, cp, cr,
           c0, c0x, z0, z0x, ut, us, rs, nl, z1, z1s, z2, nv, nvs, c2, c2o, z2o, f1,
           ssem, rsem, lsem):
    me = lax.axis_index("leaf")
    leaf, dim = points.shape
    rank = lift.shape[0]
    quarter = rank // 4
    head = leaf * 3 // 4
    sixteenth = rank // 16
    nodes = n // 16
    slot = me % 4
    group = me // 4 % 4
    part = me % 16
    node = me // 16
    step = leaf // CHUNKS

    def flip(bits):
        if bits == 1:
            return me + 1 - 2 * (me % 2)
        if bits == 2:
            return me + 2 - 4 * (me // 2 % 2)
        if bits == 3:
            return me - slot + 3 - slot
        if bits == 4:
            return me + 4 - 8 * (me // 4 % 2)
        if bits == 8:
            return me + 8 - 16 * (me // 8 % 2)
        return me - 4 * group + 4 * (3 - group)

    def flip_slot(bits):
        if bits == 1:
            return slot + 1 - 2 * (slot % 2)
        if bits == 2:
            return slot + 2 - 4 * (slot // 2)
        return 3 - slot

    others = [(node + d) % nodes * 16 + part for d in range(1, nodes)]

    barrier = pltpu.get_barrier_semaphore()
    partners = [flip(b) for b in (1, 2, 3, 4, 8, 12)] + others
    for other in partners:
        pl.semaphore_signal(barrier, inc=1, device_id=(other,), device_id_type=MESH)

    loads = [pltpu.make_async_copy(a, b, lsem.at[i]) for i, (a, b) in enumerate(
        ((charges_in, charges), (bases_in, bases), (points_in, points)))]
    for copy in loads:
        copy.start()
    count = [0]
    started = []

    def send(src, dst, device):
        i = count[0]
        count[0] += 1
        copy = pltpu.make_async_remote_copy(
            src_ref=src, dst_ref=dst, send_sem=ssem.at[i], recv_sem=rsem.at[i],
            device_id=(device,), device_id_type=MESH)
        copy.start()
        started.append(copy)
        return copy

    mine = pl.ds(pl.multiple_of(slot * quarter, quarter), quarter)
    mine16 = pl.ds(pl.multiple_of(part * sixteenth, sixteenth), sixteenth)
    mine64 = pl.ds(pl.multiple_of(group * quarter, quarter), quarter)
    z1[mine, :] = znode[...].astype(BF16)
    nl[mine, :] = nlift[...].astype(BF16)
    z2[mine16, :] = ztop[...].astype(BF16)
    z0[...] = zleaf[...].astype(BF16)
    pl.semaphore_wait(barrier, len(partners))

    def at_slot(bits):
        where = flip_slot(bits) if bits else slot
        return pl.ds(pl.multiple_of(where * quarter, quarter), quarter)

    far16 = pl.ds(pl.multiple_of(flip(2) % 16 * sixteenth, sixteenth), sixteenth)
    phase_a2 = [send(z1.at[mine, :], z1.at[mine, :], flip(2)),
                send(nl.at[mine, :], nl.at[mine, :], flip(2)),
                send(z2.at[mine16, :], z2.at[mine16, :], flip(2))]
    top, rest = pl.ds(0, head), pl.ds(head, leaf - head)
    points_two = send(points_in.at[top, :], p2.at[top, :], flip(2))
    phase_a = [send(z1.at[mine, :], z1.at[mine, :], flip(1)),
               send(nl.at[mine, :], nl.at[mine, :], flip(1)),
               send(z2.at[mine16, :], z2.at[mine16, :], flip(1))]
    points_one = send(points_in, p1, flip(1))
    loads[0].wait()

    def permute(block, carry):
        rows = pl.ds(pl.multiple_of(block * 128, 128), 128)
        index = jnp.broadcast_to(order[0:1, rows].astype(F32), (128, 128)).T
        lane = lax.broadcasted_iota(jnp.int32, (128, 128), 1).astype(F32)
        chosen = jnp.concatenate(
            [jnp.where(index == lane + 128.0 * j, 1.0, 0.0).astype(BF16) for j in range(leaf // 128)], 1)
        rhs[rows, :] = mm(chosen, charges[...]).astype(BF16)
        return carry

    lax.fori_loop(0, leaf // 128, permute, 0)

    loads[1].wait()
    own = mm(rhs[...], bases[...], 0, 0).astype(BF16)
    c0[...] = own
    up = mm(own, lift[...].astype(BF16))
    ut[...] = up.astype(BF16)
    up_near = send(ut.at[at_slot(1), :], rs.at[0], flip(1))
    up_cross = send(ut.at[at_slot(3), :], rs.at[1], flip(1))
    rhs_one = send(rhs, r1, flip(1))
    for copy in phase_a2:
        copy.wait_recv()
    phase_a.append(send(z1.at[at_slot(2), :], z1.at[at_slot(2), :], flip(1)))
    phase_a.append(send(nl.at[at_slot(2), :], nl.at[at_slot(2), :], flip(1)))
    phase_a.append(send(z2.at[far16, :], z2.at[far16, :], flip(1)))
    rhs_two = []

    def send_chunk(c):
        rows = pl.ds(c * step, step)
        rhs_two.append(send(rhs.at[rows, :], r2.at[rows, :], flip(2)))

    loads[2].wait()
    up_cross.wait_recv()
    us[...] = (ut[at_slot(2), :].astype(F32) + rs[1].astype(F32)).astype(BF16)
    up_two = send(us, rs.at[2], flip(2))
    points_rest = send(points_in.at[rest, :], p2.at[rest, :], flip(2))
    send_chunk(0)
    send_chunk(1)
    phase_far = []
    for b in (1, 2):
        phase_far.append(send(c0, c0x.at[b - 1], flip(b)))
        phase_far.append(send(z0, z0x.at[b - 1], flip(b)))
    for c in range(2, EARLY):
        send_chunk(c)

    def augment(block, carry):
        rows = pl.ds(pl.multiple_of(block * ROWS, ROWS), ROWS)
        p = points[rows, :]
        laug[rows, 0:dim] = (p.astype(F32) * (4.0 / dim)).astype(BF16)
        laug[rows, dim:] = norm_lanes(p, -2.0 / dim, -2.0 / dim, False)
        raug[rows, 0:dim] = p
        raug[rows, dim:] = norm_lanes(p, 1.0, 1.0, True)
        return carry

    lax.fori_loop(0, leaf // ROWS, augment, 0)

    def tiles(rows, right, width):
        left = laug[rows, :]
        return jnp.concatenate(
            [jnp.exp(mm(left, right[j:j + 512, :], 1, 1)).astype(BF16) for j in range(0, width, 512)], 1)

    def own_tile(block, carry):
        rows = pl.ds(pl.multiple_of(block * ROWS, ROWS), ROWS)
        acc[rows, :] = mm(tiles(rows, raug, leaf), rhs[...])
        return carry

    blocks = leaf // ROWS
    for copy in phase_a:
        copy.wait_recv()
    phase_b = []
    for i, b in enumerate((4, 8, 12)):
        phase_b.append(send(z1, z1s.at[i], flip(b)))
        phase_b.append(send(z2.at[mine64, :], z2.at[mine64, :], flip(b)))

    lax.fori_loop(0, blocks // 2, own_tile, 0)

    up_near.wait_recv()
    up_two.wait_recv()
    total = ut[mine, :].astype(F32) + rs[0].astype(F32) + rs[2].astype(F32)
    nv[0] = total.astype(BF16)
    lifted = mm(total.astype(BF16), nl[...])
    nv[1] = lifted.astype(BF16)
    phase_two = [send(nv, nvs.at[i], flip(b)) for i, b in enumerate((4, 8, 12))]
    points_two.wait_recv()
    points_three = [send(p2.at[top, :], p3.at[top, :], flip(1))]

    lax.fori_loop(blocks // 2, blocks, own_tile, 0)

    for copy in phase_b:
        copy.wait_recv()
    for copy in phase_two:
        copy.wait_recv()
    for i in range(3):
        lifted = lifted + nvs[i, 1].astype(F32)
    c2[...] = lifted.astype(BF16)
    phase_top = []
    for d, other in enumerate(others):
        phase_top.append(send(c2, c2o.at[d], other))
        phase_top.append(send(z2, z2o.at[d], other))
    points_rest.wait_recv()
    points_three.append(send(p2.at[rest, :], p3.at[rest, :], flip(1)))

    side = mm(nvs[0, 0], couple(z1s[0], z1[...]))
    for i in (1, 2):
        side = side + mm(nvs[i, 0], couple(z1s[i], z1[...]))

    first = near[0, 0] - me
    second = near[0, 1] - me
    one = 1 - 2 * (me % 2)
    near_one = jnp.logical_or(first == one, second == one)

    def choose(a, b):
        return jnp.where(near_one, a.astype(F32), b.astype(F32)).astype(BF16)

    phase_rhs = []

    def relay(c):
        rhs_two[c].wait_recv()
        rows = pl.ds(c * step, step)
        phase_rhs.append(send(r2.at[rows, :], r3.at[rows, :], flip(1)))

    def near_chunk(c, final):
        rows = pl.ds(c * step, step)
        phase_rhs[c].wait_recv()
        picked = choose(p1[rows, :], p2[rows, :])
        cp[0:step, 0:dim] = picked
        cp[0:step, dim:] = norm_lanes(picked, 1.0, 1.0, True)
        diagonal = p3[rows, :]
        cp[step:, 0:dim] = diagonal
        cp[step:, dim:] = norm_lanes(diagonal, 1.0, 1.0, True)
        cr[0:step, :] = choose(r1[rows, :], r2[rows, :])
        cr[step:, :] = r3[rows, :]

        def body(block, carry):
            rows = pl.ds(pl.multiple_of(block * ROWS, ROWS), ROWS)
            value = acc[rows, :] + mm(tiles(rows, cp, 2 * step), cr[...])
            if final:
                out[rows, :] = value.astype(BF16)
            else:
                acc[rows, :] = value
            return carry

        lax.fori_loop(0, blocks, body, 0, unroll=2)

    relay(0)
    rhs_one.wait_recv()
    points_one.wait_recv()
    for copy in points_three:
        copy.wait_recv()
    relay(1)
    near_chunk(0, False)
    for copy in phase_top:
        copy.wait_recv()
    field = mm(c2o[0], couple(z2o[0], z2[...]))
    for d in range(1, nodes - 1):
        field = field + mm(c2o[d], couple(z2o[d], z2[...]))
    field1 = side + mm(field.astype(BF16), nl[...], 1, 1)
    f1[mine, :] = field1.astype(BF16)
    down_two = send(f1.at[mine, :], f1.at[mine, :], flip(2))
    phase_down = [send(f1.at[mine, :], f1.at[mine, :], flip(1))]
    for c in range(EARLY, CHUNKS):
        send_chunk(c)
    for c in range(2, CHUNKS):
        relay(c)
        near_chunk(c - 1, False)
        if c == CHUNKS - 2:
            down_two.wait_recv()
            phase_down.append(send(f1.at[at_slot(2), :], f1.at[at_slot(2), :], flip(1)))
        if c == CHUNKS - 1:
            for copy in phase_far:
                copy.wait_recv()
            for copy in phase_down:
                copy.wait_recv()
            far_z = choose(z0x[1], z0x[0])
            far_c = choose(c0x[1], c0x[0])
            field0 = mm(far_c, couple(far_z, z0[...])) + mm(f1[...], lift[...].astype(BF16), 1, 1)
            c0x[0] = field0.astype(BF16)

            def descend(block, carry):
                rows = pl.ds(pl.multiple_of(block * ROWS, ROWS), ROWS)
                acc[rows, :] += mm(bases[rows, :], c0x[0], 1, 1)
                return carry

            lax.fori_loop(0, blocks, descend, 0)
    near_chunk(CHUNKS - 1, True)
    for copy in started:
        copy.wait_send()


def per_device(n, near, points, charges, order, bases, lift, nlift, zleaf, znode, ztop):
    leaf, dim = points.shape
    nrhs = charges.shape[1]
    rank = lift.shape[0]
    quarter = rank // 4
    nodes = n // 16
    copies = 8 + 2 + 1 + 3 + 2 + CHUNKS + 4 + 6 + 3 + 2 + 2 * (nodes - 1) + CHUNKS + 3
    v = pltpu.VMEM
    vmem = pl.BlockSpec(memory_space=pltpu.VMEM)
    return pl.pallas_call(
        functools.partial(kernel, n),
        out_shape=jax.ShapeDtypeStruct((leaf, nrhs), BF16),
        in_specs=[pl.BlockSpec(memory_space=pltpu.SMEM)] + [pl.BlockSpec(memory_space=pl.ANY)] * 3 + [vmem] * 6,
        out_specs=vmem,
        scratch_shapes=[
            v((leaf, dim), BF16), v((leaf, nrhs), BF16), v((leaf, rank), BF16),
            v((leaf, nrhs), BF16), v((leaf, 2 * dim), BF16), v((leaf, 2 * dim), BF16),
            v((leaf, nrhs), F32),
            v((leaf, dim), BF16), v((leaf, dim), BF16), v((leaf, dim), BF16),
            v((leaf, nrhs), BF16), v((leaf, nrhs), BF16), v((leaf, nrhs), BF16),
            v((2 * leaf // CHUNKS, 2 * dim), BF16), v((2 * leaf // CHUNKS, nrhs), BF16),
            v((nrhs, rank), BF16), v((2, nrhs, rank), BF16),
            v((rank, dim), BF16), v((2, rank, dim), BF16),
            v((nrhs, rank), BF16), v((quarter, rank), BF16), v((3, quarter, rank), BF16),
            v((rank, rank), BF16), v((rank, dim), BF16), v((3, rank, dim), BF16),
            v((rank, dim), BF16),
            v((2, quarter, rank), BF16), v((3, 2, quarter, rank), BF16),
            v((quarter, rank), BF16), v((nodes - 1, quarter, rank), BF16),
            v((nodes - 1, rank, dim), BF16), v((nrhs, rank), BF16),
            pltpu.SemaphoreType.DMA((copies,)), pltpu.SemaphoreType.DMA((copies,)),
            pltpu.SemaphoreType.DMA((3,)),
        ],
        compiler_params=pltpu.CompilerParams(
            collective_id=0, has_side_effects=True, vmem_limit_bytes=60 * 1024 * 1024),
    )(near, points, charges, bases, order, lift, nlift, zleaf, znode, ztop)


def solution(mesh):
    n = mesh.shape["leaf"]

    def body(points, charges, order, near, bases, lift, nlift, zleaf, znode, ztop):
        return per_device(n, near, points, charges, order, bases, lift, nlift, zleaf, znode, ztop)

    return jax.shard_map(
        body, mesh=mesh, in_specs=(P("leaf", None),) * 10, out_specs=P("leaf", None), check_vma=False)
```
